512 devices in a mesh: ind: 16 (over y, x), blk: 32 (over z, core).
Axes of the slice: x: 4, y: 4, z: 16, core: 2. Of those that a mesh axis runs over, the one named last changes fastest.
Arguments:
- dosage: bfloat16 [8192, 32768], P('ind', 'blk'), may hold values from 0 to 2
- residual: float32 [8192], P('ind'), may hold values from -9 to 9
- pairs: int32 [512, 2], P('blk'), may hold values from 0 to 127, as said below
- counts: int32 [32], P('blk'), may hold values from 12 to 16, as said below
Outputs:
- scores: bfloat16 [256, 512, 256], P('ind', 'blk')
The draws below stay inside these ranges and needn't reach their ends.
Inputs may be any that keep to these rules, and one draw needn't show every extreme that they name: For slot p, pairs[p, 0] is one of the blocks p div 16 * 4 to p div 16 * 4 + 3; the live slots of one owner have second blocks pairs[p, 1] with distinct values of pairs[p, 1] div 4. `counts`: some owner has exactly 16 live slots.
All inputs are finite; a program needn't handle non-finite values.
Results may differ from the reference program's by a relative error of at most 0.018.
Values may be sent and summed in bfloat16 or wider, within the bound.
No kernel may reach another device: no remote copies, remote signals or barrier semaphores. Data moves between devices by JAX's collectives and lax.ppermute only.
A program may use at most 64 MiB of HBM per device.

```python
import math
import jax
import jax.numpy as jnp
from jax import lax

B = 256
IND_DEV = 512
BLK_DEV = 4
CAP = 16
IND = 8192
NB = 128
SLOTS = 512
N_IND = 16
N_BLK = 32


def draw_dosage(key, part):
    freq_key, value_key = jax.random.split(key)
    columns = NB * B
    freq = jnp.exp(jax.random.uniform(freq_key, (columns,), jnp.float32, math.log(0.1), 0.0))
    base = jax.random.uniform(value_key, (IND, columns), jnp.float32, 0.0, 1.0)
    return (2.0 * freq[None, :] * base).astype(jnp.bfloat16)


def draw_residual(key, part):
    scale_key, value_key = jax.random.split(key)
    scale = jnp.exp(jax.random.uniform(scale_key, (IND,), jnp.float32, math.log(0.3), math.log(3.0)))
    value = jnp.clip(jax.random.normal(value_key, (IND,), jnp.float32), -3.0, 3.0)
    return value * scale


def draw_pairs(key, part):
    first_key, order_key, second_key = jax.random.split(key, 3)
    slot_ids = jnp.arange(SLOTS, dtype=jnp.int32)
    owner = slot_ids // CAP
    first = owner * BLK_DEV + jax.random.randint(first_key, (SLOTS,), 0, BLK_DEV, dtype=jnp.int32)
    owner_keys = jax.random.split(order_key, N_BLK)
    orders = jax.vmap(lambda k: jax.random.permutation(k, N_BLK))(owner_keys)
    holders = orders[:, :CAP].reshape(SLOTS).astype(jnp.int32)
    second = holders * BLK_DEV + jax.random.randint(second_key, (SLOTS,), 0, BLK_DEV, dtype=jnp.int32)
    return jnp.stack([first, second], axis=1).astype(jnp.int32)


def draw_counts(key, part):
    size_key, pick_key = jax.random.split(key)
    lowest = CAP - CAP // 4
    values = jax.random.randint(size_key, (N_BLK,), lowest, CAP + 1, dtype=jnp.int32)
    chosen = jax.random.randint(pick_key, (), 0, N_BLK, dtype=jnp.int32)
    values = jnp.where(jnp.arange(N_BLK, dtype=jnp.int32) == chosen, CAP, values)
    return values.astype(jnp.int32)


def setup_inputs(seed: int = 0) -> dict:
    streams_of = jax.random.split(jax.random.key(seed), 5)
    dosage = draw_dosage(jax.random.fold_in(streams_of[4], 71), 0)
    residual = draw_residual(jax.random.fold_in(streams_of[4], 71), 0)
    pairs = draw_pairs(jax.random.fold_in(streams_of[4], 71), 0)
    counts = draw_counts(jax.random.fold_in(streams_of[4], 71), 0)
    return {"dosage": dosage, "residual": residual, "pairs": pairs, "counts": counts}


EPSILON = 1e-05

def group_sum(left, right):
    left_groups = left.reshape(N_IND, IND_DEV, B).astype(jnp.float32)
    right_groups = right.reshape(N_IND, IND_DEV, B).astype(jnp.float32)
    partial_terms = jnp.einsum('gna,gnc->gac', left_groups, right_groups).astype(jnp.bfloat16)
    partial_terms = lax.optimization_barrier(partial_terms)
    return lax.optimization_barrier(jnp.sum(partial_terms.astype(jnp.float32), axis=0))

def reference(dosage, residual, pairs, counts):
    weighted = (residual[:, None] * dosage.astype(jnp.float32)).astype(jnp.bfloat16)
    weighted_sq = (weighted.astype(jnp.float32) ** 2).astype(jnp.bfloat16)
    dosage_sq = (dosage.astype(jnp.float32) ** 2).astype(jnp.bfloat16)
    slot_ids = jnp.arange(N_BLK * CAP, dtype=jnp.int32)
    live = slot_ids % CAP < jnp.take(counts, slot_ids // CAP)

    def one_slot(index):
        first = (pairs[index, 0] * B).astype(jnp.int32)
        second = (pairs[index, 1] * B).astype(jnp.int32)
        left = lax.dynamic_slice_in_dim(weighted, first, B, 1)
        left_sq = lax.dynamic_slice_in_dim(weighted_sq, first, B, 1)
        right = lax.dynamic_slice_in_dim(dosage, second, B, 1)
        right_sq = lax.dynamic_slice_in_dim(dosage_sq, second, B, 1)
        cross = group_sum(left, right)
        spread = group_sum(left_sq, right_sq)
        ratio = cross / jnp.sqrt(spread + EPSILON * IND)
        return jnp.where(live[index], ratio, jnp.float32(0.0)).astype(jnp.bfloat16)
    tiles = lax.map(one_slot, slot_ids)
    return jnp.transpose(tiles, (1, 0, 2))
```

```python
import functools

import jax
import jax.numpy as jnp
from jax import lax
from jax.experimental import pallas as pl
from jax.experimental.pallas import tpu as pltpu
from jax.sharding import Mesh
from jax.sharding import PartitionSpec as P

B = 256
EPSILON = 1e-05


def tile_kernel(cells, ring, table, place, residual, *refs):
    count = len(cells)
    out = refs[2 * count]
    parts = out.shape[0]
    for j in range(count):
        a_ref, c_ref = refs[2 * j], refs[2 * j + 1]
        entry = table[entry_at(cells[j], ring, place)]

        @pl.when(entry > 0)
        def _(a_ref=a_ref, c_ref=c_ref, j=j):
            weighted = (residual[...] * a_ref[...].astype(jnp.float32)).astype(jnp.bfloat16)
            right = c_ref[...]
            over_rows = (((0,), (0,)), ((), ()))
            cross = lax.dot_general(
                weighted, right, over_rows, preferred_element_type=jnp.float32
            )
            spread = lax.dot_general(
                weighted * weighted, right * right, over_rows, preferred_element_type=jnp.float32
            )
            out[:, j, 0] = cross.astype(jnp.bfloat16).reshape(parts, B // parts, B)
            out[:, j, 1] = spread.astype(jnp.bfloat16).reshape(parts, B // parts, B)

        @pl.when(entry == 0)
        def _(j=j):
            out[:, j] = jnp.zeros((parts, 2, B // parts, B), jnp.bfloat16)


def entry_at(cell, ring, place):
    distance, to_owner, other = cell
    owner = lax.rem(place[0] + (to_owner % ring), ring)
    core = place[1] if not other else 1 - place[1]
    return (owner * ring + (distance % ring)) * 2 + core


def tiles(cells, ring, parts, table, place, residual, operands):
    rows = residual.shape[0]

    def first_map(cell, i, table, place):
        entry = table[entry_at(cell, ring, place)]
        return (0, jnp.maximum(entry - 1, 0) // 4)

    def second_map(cell, i, table, place):
        entry = table[entry_at(cell, ring, place)]
        return (0, lax.rem(jnp.maximum(entry - 1, 0), 4))

    specs, arrays = [], []
    for cell, (a, c) in zip(cells, operands):
        specs.append(pl.BlockSpec((rows, B), functools.partial(first_map, cell)))
        specs.append(pl.BlockSpec((rows, B), functools.partial(second_map, cell)))
        arrays += [a, c]
    shape = (parts, len(cells), 2, B // parts, B)
    return pl.pallas_call(
        functools.partial(tile_kernel, cells, ring),
        out_shape=jax.ShapeDtypeStruct(shape, jnp.bfloat16),
        grid_spec=pltpu.PrefetchScalarGridSpec(
            num_scalar_prefetch=2,
            grid=(1,),
            in_specs=[pl.BlockSpec((rows, 1), lambda i, t, p: (0, 0))] + specs,
            out_specs=pl.BlockSpec(shape, lambda i, t, p: (0, 0, 0, 0, 0)),
        ),
        cost_estimate=pl.CostEstimate(
            flops=len(cells) * 4 * rows * B * B,
            bytes_accessed=len(cells) * (2 * rows * B * 2 + 2 * B * B * 2),
            transcendentals=0,
        ),
        compiler_params=pltpu.CompilerParams(vmem_limit_bytes=60 << 20),
    )(table, place, residual, *arrays)


def on_device(dosage, residual, pairs, counts):
    ring = lax.axis_size("z")
    parts = lax.axis_size("ind")
    chip, core = lax.axis_index("z"), lax.axis_index("core")
    total_rows = dosage.shape[0] * parts
    local_blocks = dosage.shape[1] // B
    slot_count = pairs.shape[0]

    live = jnp.arange(slot_count, dtype=jnp.int32) < counts[0]
    first_local = pairs[:, 0] - (chip * 2 + core) * local_blocks
    second_local = pairs[:, 1] % local_blocks
    holder = pairs[:, 1] // local_blocks
    away = (holder // 2 - chip) % ring
    position = away * 2 + holder % 2
    wanted = (position[:, None] == jnp.arange(2 * ring, dtype=jnp.int32)[None, :]) & live[:, None]
    code = 1 + first_local * local_blocks + second_local
    row = jnp.sum(jnp.where(wanted, code[:, None], 0), axis=0)
    table = lax.all_gather(row, "z", axis=0, tiled=True)
    place = jnp.stack([chip, core]).astype(jnp.int32)
    column = residual[:, None]

    def shift(x, by):
        return lax.ppermute(x, "z", [(s, (s + by) % ring) for s in range(ring)])

    def swap(x):
        return lax.ppermute(x, "core", [(0, 1), (1, 0)])

    hops = ring // 4
    below, above = [dosage], [dosage]
    here = swap(dosage)
    below_other, above_other = [here], [here]
    results = {}
    for h in range(1, hops + 1):
        below.append(shift(below[h - 1], 1))
        above.append(shift(above[h - 1], -1))
        last = h == hops
        if not last:
            below_other.append(swap(below[h]))
        above_other.append(swap(above[h]))
        cells, operands = [], []

        def add(distance, to_owner, a, c, c_other):
            cells.append((distance, to_owner, False))
            operands.append((a, c))
            cells.append((distance, to_owner, True))
            operands.append((a, c_other))

        if h == 1:
            add(0, 0, dosage, dosage, here)
        add(2 * h - 1, -h, below[h], above[h - 1], above_other[h - 1])
        add(2 * h, -h, below[h], above[h], above_other[h])
        add(1 - 2 * h, h, above[h], below[h - 1], below_other[h - 1])
        if not last:
            add(-2 * h, h, above[h], below[h], below_other[h])
        partial = tiles(tuple(cells), ring, parts, table, place, column, operands)
        summed = lax.psum_scatter(partial, "ind", scatter_dimension=0, tiled=True)[0]
        summed = summed.astype(jnp.float32)
        scores = summed[:, 0] / jnp.sqrt(summed[:, 1] + EPSILON * total_rows)
        scores = scores.astype(jnp.bfloat16)
        at = 0
        if h == 1:
            results[0] = scores[0:2]
            at = 2
        back = shift(scores[at : at + 4], -h)
        results[2 * h - 1], results[2 * h] = back[0:2], back[2:4]
        at += 4
        back = shift(scores[at:], h)
        results[1 - 2 * h] = back[0:2]
        if not last:
            results[-2 * h] = back[2:4]
    found = jnp.concatenate([results[d if d <= 2 * hops else d - ring] for d in range(ring)], axis=0)
    index = away * 2 + jnp.where(holder % 2 == core, 0, 1)
    picked = jnp.take(found, index, axis=0)
    picked = jnp.where(live[:, None, None], picked, jnp.bfloat16(0.0))
    return jnp.transpose(picked, (1, 0, 2))


def solution(mesh):
    devices = mesh.devices.reshape(mesh.shape["ind"], mesh.shape["blk"] // 2, 2)
    torus = Mesh(devices, ("ind", "z", "core"))
    owners = ("z", "core")
    placed = (P("ind", owners), P("ind"), P(owners, None), P(owners))
    return jax.shard_map(
        on_device, mesh=torus, in_specs=placed, out_specs=P("ind", owners, None), check_vma=False
    )
```

```python
import functools

import jax
import jax.numpy as jnp
from jax import lax
from jax.experimental import pallas as pl
from jax.experimental.pallas import tpu as pltpu
from jax.sharding import Mesh
from jax.sharding import PartitionSpec as P

B = 256
EPSILON = 1e-05
RING = ("z", "core")


def entry_at(cell, ring, place):
    away, back, first_other, second_other = cell
    chip, core = place[0], place[1]
    sign = 1 - 2 * core
    owner = lax.rem(chip - sign * back + ring, ring)
    distance = lax.rem(sign * away + ring, ring)
    first = 1 - core if first_other else core
    second = 1 - core if second_other else core
    return ((owner * 2 + first) * ring + distance) * 2 + second


def tile_kernel(cells, where, ring, table, place, residual, *refs):
    out = refs[-1]
    parts = out.shape[0]
    depth = B // parts
    for j, (cell, (a_at, c_at)) in enumerate(zip(cells, where)):
        entry = table[entry_at(cell, ring, place)]
        rows = slice(2 * j * depth, 2 * (j + 1) * depth)

        @pl.when(entry > 0)
        def _(a_ref=refs[a_at], c_ref=refs[c_at], j=j, entry=entry):
            first = pl.multiple_of((entry - 1) // 4 * B, B)
            second = pl.multiple_of(lax.rem(entry - 1, 4) * B, B)
            left = a_ref[:, pl.ds(first, B)].astype(jnp.float32)
            weighted = (residual[...] * left).astype(jnp.bfloat16)
            right = c_ref[:, pl.ds(second, B)]
            over_rows = (((0,), (0,)), ((), ()))
            cross = lax.dot_general(
                weighted, right, over_rows, preferred_element_type=jnp.float32
            )
            spread = lax.dot_general(
                weighted * weighted, right * right, over_rows, preferred_element_type=jnp.float32
            )
            cross = cross.astype(jnp.bfloat16).reshape(parts, depth, B)
            spread = spread.astype(jnp.bfloat16).reshape(parts, depth, B)
            out[:, 2 * j * depth : (2 * j + 1) * depth, :] = cross
            out[:, (2 * j + 1) * depth : (2 * j + 2) * depth, :] = spread

        @pl.when(entry == 0)
        def _(rows=rows):
            out[:, rows, :] = jnp.zeros((parts, 2 * depth, B), jnp.bfloat16)


def tiles(cells, operands, ring, parts, table, place, residual):
    arrays, where = [], []
    for pair in operands:
        spots = []
        for x in pair:
            spot = next((i for i, y in enumerate(arrays) if y is x), len(arrays))
            if spot == len(arrays):
                arrays.append(x)
            spots.append(spot)
        where.append(tuple(spots))
    rows = residual.shape[0]
    shape = (parts, len(cells) * 2 * (B // parts), B)
    smem = pl.BlockSpec(memory_space=pltpu.SMEM)
    vmem = pl.BlockSpec(memory_space=pltpu.VMEM)
    return pl.pallas_call(
        functools.partial(tile_kernel, cells, where, ring),
        out_shape=jax.ShapeDtypeStruct(shape, jnp.bfloat16),
        in_specs=[smem, smem, vmem] + [vmem] * len(arrays),
        out_specs=vmem,
        cost_estimate=pl.CostEstimate(
            flops=len(cells) * 4 * rows * B * B,
            bytes_accessed=len(cells) * (2 * rows * B * 2 + 2 * B * B * 2),
            transcendentals=0,
        ),
        compiler_params=pltpu.CompilerParams(vmem_limit_bytes=24 << 20),
    )(table, place, residual, *arrays)


def on_device(dosage, residual, pairs, counts):
    ring = lax.axis_size("z")
    parts = lax.axis_size("ind")
    chip, core = lax.axis_index("z"), lax.axis_index("core")
    total_rows = dosage.shape[0] * parts
    local_blocks = dosage.shape[1] // B
    slot_count = pairs.shape[0]
    depth = B // parts

    def move(x, by, cross=False):
        perm = []
        for z in range(ring):
            for k in range(2):
                to = (z + (by if k == 0 else -by)) % ring
                perm.append((z * 2 + k, to * 2 + (1 - k if cross else k)))
        return lax.ppermute(x, RING, perm)

    def swap(x):
        return move(x, 0, True)

    live = jnp.arange(slot_count, dtype=jnp.int32) < counts[0]
    first_local = pairs[:, 0] - (chip * 2 + core) * local_blocks
    second_local = pairs[:, 1] % local_blocks
    holder = pairs[:, 1] // local_blocks
    away = (holder // 2 - chip) % ring
    position = away * 2 + holder % 2
    wanted = (position[:, None] == jnp.arange(2 * ring, dtype=jnp.int32)[None, :]) & live[:, None]
    code = 1 + first_local * local_blocks + second_local
    row = jnp.sum(jnp.where(wanted, code[:, None], 0), axis=0)
    rows = jnp.broadcast_to(row[None, :], (2 * ring, 2 * ring))
    table = lax.all_to_all(rows, RING, 0, 0, tiled=True).reshape(-1)
    place = jnp.stack([chip, core]).astype(jnp.int32)
    column = residual[:, None]

    hops = ring // 4
    own, other = [dosage], [swap(dosage)]
    far_own, far_other = [dosage], [other[0]]
    near, cross = {}, {}
    for h in range(0, hops + 1):
        cells, operands = [], []
        if h == 0:
            cells = [(0, 0, False, False), (0, 0, False, True)]
            operands = [(dosage, dosage), (dosage, other[0])]
        else:
            own.append(move(own[h - 1], 1))
            other.append(move(other[h - 1], 1))
            far_other.append(swap(own[h]))
            far_own.append(swap(other[h]))
            for first_other in (False, True):
                a = other[h] if first_other else own[h]
                for away_by, at in ((2 * h - 1, h - 1), (2 * h, h)):
                    if away_by == 2 * hops and first_other:
                        continue
                    for second_other in (False, True):
                        c = far_other[at] if second_other else far_own[at]
                        cells.append((away_by, h, first_other, second_other))
                        operands.append((a, c))
        partial = tiles(tuple(cells), operands, ring, parts, table, place, column)
        arrived = lax.all_to_all(partial, "ind", 0, 0, tiled=True)
        summed = jnp.sum(arrived.astype(jnp.float32), axis=0)
        summed = summed.reshape(len(cells), 2, depth, B)
        scores = summed[:, 0] / jnp.sqrt(summed[:, 1] + EPSILON * total_rows)
        scores = scores.astype(jnp.bfloat16)
        if h == 0:
            near[0] = scores
            continue
        near[h] = move(scores[:4], -h)
        cross[h] = move(scores[4:], -h, True)
    found = jnp.concatenate(
        [near[h] for h in range(hops + 1)]
        + [jnp.concatenate([cross[h][2:4], cross[h][0:2]]) if h < hops else cross[h][0:2] for h in range(hops, 0, -1)],
        axis=0,
    )
    ahead = jnp.where(core == 0, away, -away) % ring
    unlike = (holder % 2 != core).astype(jnp.int32)
    index = ahead * 2 + jnp.where(ahead <= 2 * hops, unlike, 1 - unlike)
    picked = jnp.take(found, index, axis=0)
    picked = jnp.where(live[:, None, None], picked, jnp.bfloat16(0.0))
    return jnp.transpose(picked, (1, 0, 2))


def solution(mesh):
    devices = mesh.devices.reshape(mesh.shape["ind"], mesh.shape["blk"] // 2, 2)
    torus = Mesh(devices, ("ind", *RING))
    placed = (P("ind", RING), P("ind"), P(RING, None), P(RING))
    return jax.shard_map(
        on_device, mesh=torus, in_specs=placed, out_specs=P("ind", RING, None), check_vma=False
    )
```

```python
import functools

import jax
import jax.numpy as jnp
from jax import lax
from jax.experimental import pallas as pl
from jax.experimental.pallas import tpu as pltpu
from jax.sharding import Mesh
from jax.sharding import PartitionSpec as P


B = 256
EPSILON = 1e-05
RING = ("z", "core")
INFO = 16


def column_of(cell, ring, place):
    away, _, second_other = cell
    core = place[1]
    distance = lax.rem((1 - 2 * core) * away + ring, ring)
    return distance * 2 + (1 - core if second_other else core)


def tile_kernel(cells, where, ring, place, residual, info_ref, *refs):
    out = refs[-1]
    parts = out.shape[0]
    depth = B // parts
    count = residual.shape[0]
    entries = []
    for cell in cells:
        start = count + (0 if cell[1] else INFO)
        line = info_ref[start : start + INFO, 0:128].astype(jnp.float32)
        spot = lax.broadcasted_iota(jnp.int32, line.shape, 1) == column_of(cell, ring, place)
        entries.append(jnp.sum(jnp.where(spot, line, 0.0)).astype(jnp.int32))
    for j, (a_at, c_at) in enumerate(where):
        entry = entries[j]
        rows = slice(2 * j * depth, 2 * (j + 1) * depth)

        @pl.when(entry > 0)
        def _(a_ref=refs[a_at], c_ref=refs[c_at], j=j, entry=entry):
            first = pl.multiple_of((entry - 1) // 4 * B, B)
            second = pl.multiple_of(lax.rem(entry - 1, 4) * B, B)
            left = a_ref[0:count, pl.ds(first, B)].astype(jnp.float32)
            weighted = (residual[...] * left).astype(jnp.bfloat16)
            right = c_ref[0:count, pl.ds(second, B)]
            over_rows = (((0,), (0,)), ((), ()))
            cross = lax.dot_general(
                weighted, right, over_rows, preferred_element_type=jnp.float32
            )
            spread = lax.dot_general(
                weighted * weighted, right * right, over_rows, preferred_element_type=jnp.float32
            )
            cross = cross.astype(jnp.bfloat16).reshape(parts, depth, B)
            spread = spread.astype(jnp.bfloat16).reshape(parts, depth, B)
            out[:, 2 * j * depth : (2 * j + 1) * depth, :] = cross
            out[:, (2 * j + 1) * depth : (2 * j + 2) * depth, :] = spread

        @pl.when(entry == 0)
        def _(rows=rows):
            out[:, rows, :] = jnp.zeros((parts, 2 * depth, B), jnp.bfloat16)


def tiles(cells, operands, info, ring, parts, place, residual):
    arrays, where = [], []
    for pair in operands:
        spots = []
        for x in pair:
            spot = next((i for i, y in enumerate(arrays) if y is x), len(arrays))
            if spot == len(arrays):
                arrays.append(x)
            spots.append(spot)
        where.append(tuple(spots))
    rows = residual.shape[0]
    shape = (parts, len(cells) * 2 * (B // parts), B)
    smem = pl.BlockSpec(memory_space=pltpu.SMEM)
    vmem = pl.BlockSpec(memory_space=pltpu.VMEM)
    return pl.pallas_call(
        functools.partial(tile_kernel, cells, where, ring),
        out_shape=jax.ShapeDtypeStruct(shape, jnp.bfloat16),
        in_specs=[smem, vmem, vmem] + [vmem] * len(arrays),
        out_specs=vmem,
        cost_estimate=pl.CostEstimate(
            flops=len(cells) * 4 * rows * B * B,
            bytes_accessed=len(cells) * (2 * rows * B * 2 + 2 * B * B * 2),
            transcendentals=0,
        ),
        compiler_params=pltpu.CompilerParams(vmem_limit_bytes=24 << 20),
    )(place, residual, info, *arrays)


def scores_of(dosage, residual, pairs, counts):
    ring = lax.axis_size("z")
    parts = lax.axis_size("ind")
    chip, core = lax.axis_index("z"), lax.axis_index("core")
    total_rows = dosage.shape[0] * parts
    local_blocks = dosage.shape[1] // B
    slot_count = pairs.shape[0]
    depth = B // parts

    def move(x, by, cross=False):
        perm = []
        for z in range(ring):
            for k in range(2):
                to = (z + (by if k == 0 else -by)) % ring
                perm.append((z * 2 + k, to * 2 + (1 - k if cross else k)))
        return lax.ppermute(x, RING, perm)

    def swap(x):
        return move(x, 0, True)

    live = jnp.arange(slot_count, dtype=jnp.int32) < counts[0]
    first_local = pairs[:, 0] - (chip * 2 + core) * local_blocks
    second_local = pairs[:, 1] % local_blocks
    holder = pairs[:, 1] // local_blocks
    away = (holder // 2 - chip) % ring
    position = away * 2 + holder % 2
    wanted = (position[:, None] == jnp.arange(2 * ring, dtype=jnp.int32)[None, :]) & live[:, None]
    code = 1 + first_local * local_blocks + second_local
    row = jnp.sum(jnp.where(wanted, code[:, None], 0), axis=0)
    info = jnp.pad(row.astype(jnp.bfloat16)[None, :], ((0, INFO - 1), (0, dosage.shape[1] - 2 * ring)))
    place = jnp.stack([chip, core]).astype(jnp.int32)
    column = residual[:, None]

    hops = ring // 4
    across = swap(jnp.concatenate([dosage, info]))
    own, other = [dosage], [jnp.concatenate([across, info])]
    far_own, far_other = [dosage], [other[0]]
    near, cross = {}, {}
    for h in range(0, hops + 1):
        cells, operands = [], []
        if h == 0:
            cells = [(0, False, False), (0, False, True)]
            operands = [(dosage, dosage), (dosage, other[0])]
        else:
            own.append(move(own[h - 1], 1))
            other.append(move(other[h - 1], 1))
            far_other.append(swap(own[h]))
            far_own.append(swap(other[h]))
            for first_other in (False, True):
                a = other[h] if first_other else own[h]
                for away_by, at in ((2 * h - 1, h - 1), (2 * h, h)):
                    if away_by == 2 * hops and first_other:
                        continue
                    for second_other in (False, True):
                        c = far_other[at] if second_other else far_own[at]
                        cells.append((away_by, first_other, second_other))
                        operands.append((a, c))
        partial = tiles(tuple(cells), operands, other[h], ring, parts, place, column)
        arrived = lax.all_to_all(partial, "ind", 0, 0, tiled=True)
        summed = jnp.sum(arrived.astype(jnp.float32), axis=0)
        summed = summed.reshape(len(cells), 2, depth, B)
        scores = summed[:, 0] / jnp.sqrt(summed[:, 1] + EPSILON * total_rows)
        scores = scores.astype(jnp.bfloat16)
        if h == 0:
            near[0] = scores
            continue
        near[h] = move(scores[:4], -h)
        cross[h] = move(scores[4:], -h, True)
    found = jnp.concatenate(
        [near[h] for h in range(hops + 1)]
        + [jnp.concatenate([cross[h][2:4], cross[h][0:2]]) if h < hops else cross[h][0:2] for h in range(hops, 0, -1)],
        axis=0,
    )
    ahead = jnp.where(core == 0, away, -away) % ring
    unlike = (holder % 2 != core).astype(jnp.int32)
    index = ahead * 2 + jnp.where(ahead <= 2 * hops, unlike, 1 - unlike)
    picked = jnp.take(found, index, axis=0)
    picked = jnp.where(live[:, None, None], picked, jnp.bfloat16(0.0))
    return jnp.transpose(picked, (1, 0, 2))


def solution(mesh):
    devices = mesh.devices.reshape(mesh.shape["ind"], mesh.shape["blk"] // 2, 2)
    torus = Mesh(devices, ("ind", *RING))
    placed = (P("ind", RING), P("ind"), P(RING, None), P(RING))
    return jax.shard_map(scores_of, mesh=torus, in_specs=placed, out_specs=P("ind", RING, None), check_vma=False)
```

```python
import functools

import jax
import jax.numpy as jnp
from jax import lax
from jax.experimental import pallas as pl
from jax.experimental.pallas import tpu as pltpu
from jax.sharding import Mesh
from jax.sharding import PartitionSpec as P


B = 256
EPSILON = 1e-05
RING = ("z", "core")
INFO = 16
PACK = 4
BASE = 32


def column_of(cell, ring, place):
    away, _, second_other, _ = cell
    core = place[1]
    distance = lax.rem((1 - 2 * core) * away + ring, ring)
    return distance * 2 + (1 - core if second_other else core)


def tile_kernel(cells, where, ring, place, residual, *refs):
    out = refs[-1]
    parts = out.shape[0]
    depth = B // parts
    count = residual.shape[1]
    entries = []
    for first in range(0, len(cells), PACK):
        packed = jnp.zeros((8, 128), jnp.float32)
        for j in range(first, min(first + PACK, len(cells))):
            start = cells[j][3]
            line = refs[where[j][2]][start : start + INFO, 0:128].astype(jnp.float32)[0:8]
            spot = lax.broadcasted_iota(jnp.int32, line.shape, 1) == column_of(cells[j], ring, place)
            packed = packed + jnp.where(spot, line * float(BASE ** (j - first)), 0.0)
        total = jnp.sum(packed).astype(jnp.int32)
        for j in range(first, min(first + PACK, len(cells))):
            entries.append(lax.rem(total // BASE ** (j - first), BASE))
    for j, (a_at, c_at, _) in enumerate(where):
        entry = entries[j]
        rows = slice(2 * j * depth, 2 * (j + 1) * depth)

        @pl.when(entry > 0)
        def _(a_ref=refs[a_at], c_ref=refs[c_at], j=j, entry=entry):
            first = pl.multiple_of((entry - 1) // 4 * B, B)
            second = pl.multiple_of(lax.rem(entry - 1, 4) * B, B)
            left = a_ref[0:count, pl.ds(first, B)].T.astype(jnp.float32)
            weighted = (residual[...] * left).astype(jnp.bfloat16)
            right = c_ref[0:count, pl.ds(second, B)]
            cross = jnp.dot(weighted, right, preferred_element_type=jnp.float32)
            spread = jnp.dot(
                weighted * weighted, right * right, preferred_element_type=jnp.float32
            )
            cross = cross.astype(jnp.bfloat16).reshape(parts, depth, B)
            spread = spread.astype(jnp.bfloat16).reshape(parts, depth, B)
            out[:, 2 * j * depth : (2 * j + 1) * depth, :] = cross
            out[:, (2 * j + 1) * depth : (2 * j + 2) * depth, :] = spread

        @pl.when(entry == 0)
        def _(rows=rows):
            out[:, rows, :] = jnp.zeros((parts, 2 * depth, B), jnp.bfloat16)


def tiles(cells, operands, ring, parts, place, residual):
    arrays, where = [], []
    for triple in operands:
        spots = []
        for x in triple:
            spot = next((i for i, y in enumerate(arrays) if y is x), len(arrays))
            if spot == len(arrays):
                arrays.append(x)
            spots.append(spot)
        where.append(tuple(spots))
    rows = residual.shape[1]
    shape = (parts, len(cells) * 2 * (B // parts), B)
    smem = pl.BlockSpec(memory_space=pltpu.SMEM)
    vmem = pl.BlockSpec(memory_space=pltpu.VMEM)
    return pl.pallas_call(
        functools.partial(tile_kernel, cells, where, ring),
        out_shape=jax.ShapeDtypeStruct(shape, jnp.bfloat16),
        in_specs=[smem, vmem] + [vmem] * len(arrays),
        out_specs=vmem,
        cost_estimate=pl.CostEstimate(
            flops=len(cells) * 4 * rows * B * B,
            bytes_accessed=len(cells) * (2 * rows * B * 2 + 2 * B * B * 2),
            transcendentals=0,
        ),
        compiler_params=pltpu.CompilerParams(vmem_limit_bytes=10 << 20),
    )(place, residual, *arrays)


def scores_of(dosage, residual, pairs, counts):
    ring = lax.axis_size("z")
    parts = lax.axis_size("ind")
    chip, core = lax.axis_index("z"), lax.axis_index("core")
    total_rows = dosage.shape[0] * parts
    local_blocks = dosage.shape[1] // B
    slot_count = pairs.shape[0]
    depth = B // parts

    def move(x, by, cross=False):
        perm = []
        for z in range(ring):
            for k in range(2):
                to = (z + (by if k == 0 else -by)) % ring
                perm.append((z * 2 + k, to * 2 + (1 - k if cross else k)))
        return lax.ppermute(x, RING, perm)

    def swap(x):
        return move(x, 0, True)

    live = jnp.arange(slot_count, dtype=jnp.int32) < counts[0]
    first_local = pairs[:, 0] - (chip * 2 + core) * local_blocks
    second_local = pairs[:, 1] % local_blocks
    holder = pairs[:, 1] // local_blocks
    away = (holder // 2 - chip) % ring
    position = away * 2 + holder % 2
    wanted = (position[:, None] == jnp.arange(2 * ring, dtype=jnp.int32)[None, :]) & live[:, None]
    code = 1 + first_local * local_blocks + second_local
    row = jnp.sum(jnp.where(wanted, code[:, None], 0), axis=0)
    info = jnp.pad(row.astype(jnp.bfloat16)[None, :], ((0, INFO - 1), (0, dosage.shape[1] - 2 * ring)))
    place = jnp.stack([chip, core]).astype(jnp.int32)
    weights = residual[None, :]

    hops = ring // 4
    across = swap(jnp.concatenate([dosage, info]))
    own, other = [dosage], [jnp.concatenate([across, info])]
    ahead_info = move(info, 1)
    far_own, far_other = [dosage], [other[0]]
    count = dosage.shape[0]
    results = {}

    def exchange(cells, operands):
        partial = tiles(tuple(cells), operands, ring, parts, place, weights)
        arrived = lax.all_to_all(partial, "ind", 0, 0, tiled=True)
        summed = jnp.sum(arrived.astype(jnp.float32), axis=0)
        summed = summed.reshape(len(cells), 2, depth, B)
        scores = summed[:, 0] / jnp.sqrt(summed[:, 1] + EPSILON * total_rows)
        scores = scores.astype(jnp.bfloat16)
        for j in range(0, len(cells), 2):
            results[cells[j][:2]] = scores[j : j + 2]

    def both(away_by, first_other, a, at, table, start):
        for second_other in (False, True):
            c = far_other[at] if second_other else far_own[at]
            cells.append((away_by, first_other, second_other, start))
            operands.append((a, c, table))

    near, cross = {}, {}
    for h in range(1, hops + 1):
        own.append(move(own[h - 1], 1))
        other.append(move(other[h - 1], 1))
        cells, operands = [], []
        if h == 1:
            both(0, False, dosage, 0, other[0], count + INFO)
            both(1, False, own[1], 0, ahead_info, 0)
            exchange(cells, operands)
            near[0] = results[0, False]
            cells, operands = [], []
        far_other.append(swap(own[h]))
        far_own.append(swap(other[h]))
        for first_other in (False, True):
            a = other[h] if first_other else own[h]
            start = count + (0 if first_other else INFO)
            if h > 1 or first_other:
                both(2 * h - 1, first_other, a, h - 1, other[h], start)
            if h < hops or not first_other:
                both(2 * h, first_other, a, h, other[h], start)
        exchange(cells, operands)
        odd, even = 2 * h - 1, 2 * h
        sent = [results[odd, False], results[even, False]]
        if h < hops:
            sent.append(results[even, True])
        sent.append(results[odd, True])
        came = move(jnp.concatenate(sent), -h)
        near[h], cross[h] = came[:4], came[4:]
    crossed = swap(jnp.concatenate([cross[h] for h in range(hops, 0, -1)]))
    found = jnp.concatenate([near[h] for h in range(hops + 1)] + [crossed], axis=0)
    ahead = jnp.where(core == 0, away, -away) % ring
    unlike = (holder % 2 != core).astype(jnp.int32)
    index = ahead * 2 + jnp.where(ahead <= 2 * hops, unlike, 1 - unlike)
    picked = jnp.take(found, index, axis=0)
    picked = jnp.where(live[:, None, None], picked, jnp.bfloat16(0.0))
    return jnp.transpose(picked, (1, 0, 2))


def solution(mesh):
    devices = mesh.devices.reshape(mesh.shape["ind"], mesh.shape["blk"] // 2, 2)
    torus = Mesh(devices, ("ind", *RING))
    placed = (P("ind", RING), P("ind"), P(RING, None), P(RING))
    return jax.shard_map(scores_of, mesh=torus, in_specs=placed, out_specs=P("ind", RING, None), check_vma=False)
```
